512 devices in a mesh: ep: 128 (over y, z, core), rep: 4 (over x).
Axes of the slice: x: 4, y: 8, z: 8, core: 2. Of those that a mesh axis runs over, the one named last changes fastest.
Arguments:
- tokens: bfloat16 [2048, 3584], P('ep', 'rep'), may hold values from -6 to 6
- expert_ids: int32 [2048, 8], P('ep'), may hold values from 0 to 127, all different within a row; in each aligned block of 16 rows (0 to 15, 16 to 31, ...) at most 2 rows name the same one
- gate_weights: float32 [2048, 8], P('ep'), may hold values from 0.05 to 0.5
- up_weight: bfloat16 [128, 3584, 1024], P('ep', 'rep'), may hold values from -0.09375 to 0.09375
- down_weight: bfloat16 [128, 1024, 3584], P('ep', None, 'rep'), may hold values from -0.1875 to 0.1875
Outputs:
- mixture: bfloat16 [2048, 3584], P('ep', 'rep')
The draws below stay inside these ranges and needn't reach their ends.
Inputs may be any that keep to these rules, and one draw needn't show every extreme that they name: `expert_ids`: the 8 experts of a token differ. Within the rows of one device (each aligned block of 16 tokens) no expert is named by more than 2 tokens, a bound that some block reaches.
All inputs are finite; a program needn't handle non-finite values.
Results may differ from the reference program's by a relative error of at most 0.017.
Values may be sent and summed in bfloat16 or wider, within the bound.
A program may use at most 64 MiB of HBM per device.

```python
import math
import jax
import jax.numpy as jnp
import numpy as np
from jax import lax

D = 3584
FF = 1024
TOP = 8
TOK_EP = 16
EXPERTS = 128
TOKENS = 2048
DQ = 896
CAP = 2
N_EP = 128


def level_of(key, dims, cuts, low, top_value):
    loudness = 1.0
    for axis_at, parts in cuts:
        draws = jax.random.uniform(jax.random.fold_in(jax.random.fold_in(key, 6), axis_at), (parts,), jnp.float32, low / len(cuts), top_value / len(cuts))
        loudness = loudness * jnp.repeat(jnp.exp(draws), dims[axis_at] // parts).reshape((-1,) + (1,) * (len(dims) - 1 - axis_at))
    return loudness


def routed_block(own_key, own, number, rows, number_of, top, bound, skew):
    order = jax.random.permutation(own_key, number_of)
    heavy_load, ordinary = shares(number_of, rows * top, bound, skew, True), shares(number_of, rows * top, bound, skew, False)
    places = jnp.arange(number_of)

    def named(tallies, offset_by):
        used = int((tallies > 0).sum())
        fixed = max(1, used // 4)
        moved = fixed + (places - fixed + offset_by * (used - fixed)) % max(1, number_of - fixed)
        return jnp.zeros((number_of,), jnp.int32).at[order[jnp.where(places < fixed, places, moved)]].set(jnp.asarray(tallies, jnp.int32))

    tallies = jnp.where(number % 4 == 0, named(heavy_load, number // 4), named(ordinary, number - number // 4 - 1))
    mixed = jax.random.permutation(jax.random.fold_in(own, 3), number_of)
    donor, receiver = mixed[0:number_of // 2 * 2:2], mixed[1:number_of // 2 * 2:2]
    room = jnp.minimum(tallies[donor] - 1, bound - tallies[receiver]) // 2
    room = jnp.where((donor == order[0]) | (receiver == order[0]) | (tallies[receiver] == 0), 0, jnp.maximum(room, 0))
    moved = jax.random.randint(jax.random.fold_in(own, 4), (number_of // 2,), 0, 1 << 20) % (room + 1)
    tallies = tallies.at[donor].add(-moved).at[receiver].add(moved)
    members = jnp.searchsorted(jnp.cumsum(tallies), jnp.arange(rows * top), side="right").astype(jnp.int32)
    listing = members.reshape(top, rows).T
    listing = listing[jax.random.permutation(jax.random.fold_in(own, 1), rows)]
    offset_by = jax.random.randint(jax.random.fold_in(own, 2), (rows, 1), 0, top)
    return jnp.take_along_axis(listing, (jnp.arange(top)[None, :] + offset_by) % top, axis=1)


def shares(count, total, most, slope, full):
    portions = [(1 << 20) // math.isqrt(rank ** slope) + 1 for rank in range(1, count + 1)]
    largest = most if full else min(most, max(-(-total // count), total * portions[0] // sum(portions)))
    least = 1 if total - largest >= count - 1 else 0
    given, surplus = [largest] + [least] * (count - 1), total - largest - least * (count - 1)
    while surplus > 0:
        candidates = [i for i in range(1, count) if given[i] < largest] or [i for i in range(1, count) if given[i] < most]
        mass, budget = sum([portions[i] for i in candidates]), surplus
        for i in candidates:
            addition = min(most - given[i], max(1, budget * portions[i] // mass), surplus)
            given[i] = given[i] + addition
            surplus = surplus - addition
    return np.array(given)


def centred(own_key, shape, deviation, reach, pieces=(), kind=jnp.bfloat16):
    result = jax.random.normal(own_key, shape, jnp.float32) * deviation
    if len(pieces) > 0:
        result = level_of(own_key, shape, pieces, -0.22, 0.18) * result
    return jnp.clip(result, min=-reach, max=reach).astype(kind)


def setup_inputs(seed: int = 0) -> dict:
    splits = jax.random.split(jax.random.key(seed), 6)
    tokens = centred(splits[0], (TOKENS, D), 1.0, 6.0, ((0, 128), (1, 4)))
    expert_ids_keys = jax.random.split(jax.random.fold_in(splits[1], 1), TOKENS // TOK_EP)
    expert_ids_turns = jax.random.permutation(jax.random.fold_in(splits[1], 3), TOKENS // TOK_EP)
    expert_ids = jax.vmap(lambda own, number: routed_block(jax.random.fold_in(splits[1], 2), own, number, TOK_EP, EXPERTS, TOP, CAP, 2))(expert_ids_keys, expert_ids_turns).reshape((TOKENS, TOP))
    gate_weights = jnp.clip(0.05 + 0.45 * jax.random.uniform(splits[2], (TOKENS, TOP), jnp.float32) ** level_of(splits[2], (TOKENS, TOP), ((0, 128),), -0.2, 0.2), 0.05, 0.5)
    up_weight = centred(splits[3], (EXPERTS, D, FF), D ** -0.5, 0.09375, ((0, 128), (1, 4)))
    down_weight = centred(splits[4], (EXPERTS, FF, D), FF ** -0.5, 0.1875, ((0, 128), (2, 4)))
    return dict(tokens=tokens, expert_ids=expert_ids, gate_weights=gate_weights, up_weight=up_weight, down_weight=down_weight)


def expert_rows(inputs, up_matrix, down_matrix):
    pre = jnp.zeros((inputs.shape[0], FF), jnp.float32)
    for block in range(D // DQ):
        part = jnp.dot(inputs[:, block * DQ:(block + 1) * DQ], up_matrix[block * DQ:(block + 1) * DQ], preferred_element_type=jnp.float32)
        rounded = lax.optimization_barrier(part.astype(jnp.bfloat16))
        pre = pre + rounded.astype(jnp.float32)
    hidden = jax.nn.silu(pre).astype(jnp.bfloat16)
    return jnp.dot(hidden, down_matrix, preferred_element_type=jnp.float32).astype(jnp.bfloat16)


def reference(tokens, expert_ids, gate_weights, up_weight, down_weight):
    rows_total = TOKENS * TOP
    flat_ids = expert_ids.reshape(-1).astype(jnp.int32)
    order = jnp.argsort(flat_ids, stable=True).astype(jnp.int32)
    matches = (flat_ids[:, None] == jnp.arange(EXPERTS, dtype=jnp.int32)[None, :]).astype(jnp.int32)
    counts = jnp.sum(matches, axis=0).astype(jnp.int32)
    starts = (jnp.cumsum(counts) - counts).astype(jnp.int32)
    limit = N_EP * CAP

    def one_expert(expert):
        offsets = jnp.arange(limit, dtype=jnp.int32)
        positions = starts[expert] + offsets
        valid = offsets < counts[expert]
        row_ids = order[jnp.minimum(positions, rows_total - 1)].astype(jnp.int32)
        inputs = tokens[row_ids // TOP]
        outputs = expert_rows(inputs, up_weight[expert], down_weight[expert])
        target = jnp.where(valid, row_ids, rows_total).astype(jnp.int32)
        return outputs, target

    outputs, targets = lax.map(one_expert, jnp.arange(EXPERTS, dtype=jnp.int32))
    placed = jnp.zeros((rows_total, D), jnp.bfloat16).at[targets.reshape(-1)].set(outputs.reshape(-1, D), mode="drop")
    picked = placed.astype(jnp.float32).reshape(TOKENS, TOP, D)
    return jnp.sum(gate_weights[:, :, None] * picked, axis=1).astype(jnp.bfloat16)
```

```python
import functools

import jax
import jax.numpy as jnp
from jax import lax
from jax.experimental import pallas as pl
from jax.experimental.pallas import tpu as pltpu
from jax.sharding import PartitionSpec as P

MESH = pl.DeviceIdType.MESH
F32, BF16 = jnp.float32, jnp.bfloat16


def far_first(n):
    return sorted(range(1, n), key=lambda s: -min(s, n - s))


def dot(a, b, ca, cb):
    return lax.dot_general(a, b, (((ca,), (cb,)), ((), ())), preferred_element_type=F32)


def iota(shape, dim):
    return lax.broadcasted_iota(jnp.int32, shape, dim)


def kernel(
    side, reps, ids_hbm, gates_hbm, tok_hbm, up_hbm, down_hbm, out_ref,
    ids_v, gates_v, up_v, down_v, told, picked, inbound, part, gathered, hid, acc,
    sent, back, mixed, shares,
    s_load, s_bc, r_bc, s_pick, r_pick, s_part, r_part, s_hid, r_hid, s_out, r_out, s_mix, r_mix,
):
    top, toks = ids_v.shape
    experts = 2 * side * side
    width = tok_hbm.shape[1]
    chunks = s_part.shape[1]
    ffc = up_v.shape[1] // chunks
    lines = 2 * side
    rows = lines * lines
    e = lax.axis_index("ep")
    x = lax.axis_index("rep")
    y, z, c = e // (2 * side), (e // 2) % side, e % 2
    p, q = y * (1 - c) + z * c, z * (1 - c) + y * c
    sp = 2 * side * (1 - c) + 2 * c
    sq = 2 * (1 - c) + 2 * side * c

    def mod(v, n):
        return lax.rem(v, n)

    barrier = pltpu.get_barrier_semaphore()

    def greet(ep, rep):
        pl.semaphore_signal(barrier, inc=1, device_id=(ep, rep), device_id_type=MESH)

    for s in far_first(side):
        for core in range(2):
            greet(y * 2 * side + mod(z + s, side) * 2 + core, x)
            greet(mod(y + s, side) * 2 * side + z * 2 + core, x)
    greet(e + 1 - 2 * c, x)
    for s in far_first(reps):
        greet(e, mod(x + s, reps))

    loads = [
        pltpu.make_async_copy(ids_hbm, ids_v, s_load.at[0]),
        pltpu.make_async_copy(gates_hbm, gates_v, s_load.at[1]),
        pltpu.make_async_copy(tok_hbm, told.at[p, :, pl.ds(0, width)], s_load.at[2]),
        pltpu.make_async_copy(up_hbm.at[0], up_v, s_load.at[3]),
        pltpu.make_async_copy(down_hbm.at[0], down_v, s_load.at[4]),
    ]
    for load in loads:
        load.start()

    loads[0].wait()
    loads[1].wait()
    ids, gates = ids_v[...], gates_v[...]
    which = iota((experts, toks), 0)
    named = jnp.zeros((experts, toks), F32)
    gate = jnp.zeros((experts, toks), F32)
    for k in range(top):
        same = which == ids[k:k + 1, :]
        named = jnp.where(same, 1.0, named)
        gate = jnp.where(same, gates[k:k + 1, :], gate)
    earlier = (iota((toks, toks), 0) < iota((toks, toks), 1)).astype(BF16)
    rank = dot(named.astype(BF16), earlier, 1, 0)
    code = jnp.where(rank > 0.5, -gate, gate).astype(BF16)
    eye = (iota((experts, experts), 0) == iota((experts, experts), 1)).astype(BF16)
    told[p, :, width:] = dot(code, eye, 0, 0).astype(BF16)
    loads[2].wait()

    pl.semaphore_wait(barrier, 4 * (side - 1) + 1 + reps - 1)

    spread = []
    for s in far_first(side):
        to = mod(p + s, side)
        spread.append(pltpu.make_async_remote_copy(
            src_ref=told.at[p], dst_ref=told.at[p], send_sem=s_bc.at[s], recv_sem=r_bc.at[p],
            device_id=(to * sp + q * sq + c, x), device_id_type=MESH))
        spread[-1].start()

    def arrival(ref, sem):
        pltpu.make_async_copy(ref, ref, sem).wait()

    for s in far_first(side):
        frm = mod(p + s, side)
        arrival(told.at[frm], r_bc.at[frm])

    held = told[...].reshape(side * toks, width + experts)
    codes = held[:, width:]

    def expert_of(col):
        block = col // lines
        return p * sp + (block // 2) * sq + block % 2

    col, tok = iota((rows, side * toks), 0), iota((rows, side * toks), 1)
    sel = (expert_of(iota((rows, experts), 0)) == iota((rows, experts), 1)).astype(BF16)
    value = dot(sel, codes, 1, 1)
    sign = (1 - 2 * (col % 2)).astype(F32)
    hit = (value * sign > 0.0) & ((col % lines) // 2 == tok // toks)
    pick = jnp.where(hit, 1.0, 0.0).astype(BF16)
    picked[...] = dot(pick, held[:, :width], 1, 0).astype(BF16).reshape(lines, lines, width)

    group = c * side + q
    own = q * 2 + c
    send_pick = []
    for s in far_first(side) + [0]:
        for core in range(2):
            if s == 0 and core == 1:
                continue
            to = mod(q + s, side)
            core_to = mod(c + core, 2) if s else 1 - c
            send_pick.append(pltpu.make_async_remote_copy(
                src_ref=picked.at[to * 2 + core_to], dst_ref=inbound.at[group],
                send_sem=s_pick.at[s * 2 + core], recv_sem=r_pick.at[group],
                device_id=(p * sp + to * sq + core_to, x), device_id_type=MESH))
            send_pick[-1].start()
    inbound[group] = picked[own]

    col, tok = iota((side * toks, rows), 1), iota((side * toks, rows), 0)
    sel = (expert_of(iota((experts, rows), 1)) == iota((experts, rows), 0)).astype(BF16)
    value = dot(codes, sel, 1, 0) * (1 - 2 * (col % 2)).astype(F32)
    hit = (value > 0.0) & ((col % lines) // 2 == tok // toks)
    weight = jnp.where(hit, value, 0.0).astype(BF16)

    for s in range(1, lines):
        frm = mod(group + s, lines)
        arrival(inbound.at[frm], r_pick.at[frm])

    per = rows // reps
    loads[3].wait()
    lhs = inbound[...].reshape(rows, width)
    send_part = []
    for n in range(chunks):
        cols = pl.ds(n * ffc, ffc)
        block = dot(lhs, up_v[:, cols], 1, 0).astype(BF16).reshape(reps, per, ffc)
        part[:, :, cols] = block
        for s in far_first(reps):
            to = mod(x + s, reps)
            send_part.append(pltpu.make_async_remote_copy(
                src_ref=part.at[to, :, cols], dst_ref=gathered.at[x, :, cols],
                send_sem=s_part.at[s, n], recv_sem=r_part.at[x, n],
                device_id=(e, to), device_id_type=MESH))
            send_part[-1].start()
        gathered[x, :, cols] = part[x, :, cols]

    send_hid = []
    for n in range(chunks):
        cols = pl.ds(n * ffc, ffc)
        for s in range(1, reps):
            frm = mod(x + s, reps)
            arrival(gathered.at[frm, :, cols], r_part.at[frm, n])
        pre = gathered[0, :, cols].astype(F32)
        for r in range(1, reps):
            pre = pre + gathered[r, :, cols].astype(F32)
        hid[x, :, cols] = (pre / (1.0 + jnp.exp(-pre))).astype(BF16)
        for s in far_first(reps):
            send_hid.append(pltpu.make_async_remote_copy(
                src_ref=hid.at[x, :, cols], dst_ref=hid.at[x, :, cols],
                send_sem=s_hid.at[s, n], recv_sem=r_hid.at[x, n],
                device_id=(e, mod(x + s, reps)), device_id_type=MESH))
            send_hid[-1].start()

    loads[4].wait()
    for n in range(chunks):
        cols = pl.ds(n * ffc, ffc)
        for s in range(1, reps):
            frm = mod(x + s, reps)
            arrival(hid.at[frm, :, cols], r_hid.at[frm, n])
        term = dot(hid[:, :, cols].reshape(rows, ffc), down_v[cols, :], 1, 0)
        if n == 0:
            acc[...] = term
        elif n < chunks - 1:
            acc[...] += term
        else:
            sent[...] = (acc[...] + term).astype(BF16).reshape(lines, lines, width)

    send_out = []

    def to_relay(slot, block, place, device):
        send_out.append(pltpu.make_async_remote_copy(
            src_ref=sent.at[block], dst_ref=back.at[place], send_sem=s_out.at[slot], recv_sem=r_out.at[place],
            device_id=(device, x), device_id_type=MESH))
        send_out[-1].start()

    for s in far_first(side) + [0]:
        if s:
            to = mod(q + s, side)
            to_relay(2 * s, c * side + to, own, p * sp + to * sq + c)
        to = mod(p + s, side)
        to_relay(2 * s + 1, (1 - c) * side + to, p * 2 + c, to * sp + q * sq + 1 - c)
    back[own] = sent[group]
    for s in range(1, lines):
        frm = mod(own + s, lines)
        arrival(back.at[frm], r_out.at[frm])

    mixed[...] = dot(weight, back[...].reshape(rows, width), 1, 0).astype(BF16).reshape(side, toks, width)
    send_mix = []
    for s in far_first(side):
        to = mod(p + s, side)
        send_mix.append(pltpu.make_async_remote_copy(
            src_ref=mixed.at[to], dst_ref=shares.at[p], send_sem=s_mix.at[s], recv_sem=r_mix.at[p],
            device_id=(to * sp + q * sq + c, x), device_id_type=MESH))
        send_mix[-1].start()
    shares[p] = mixed[p]
    for s in range(1, side):
        frm = mod(p + s, side)
        arrival(shares.at[frm], r_mix.at[frm])
    total = shares[0].astype(F32)
    for k in range(1, side):
        total = total + shares[k].astype(F32)
    out_ref[...] = total.astype(BF16)

    for copy in spread + send_pick + send_part + send_hid + send_out + send_mix:
        copy.wait_send()


def local(side, reps, chunks, tokens, expert_ids, gate_weights, up_weight, down_weight):
    toks, top = expert_ids.shape
    width = tokens.shape[1]
    ff = up_weight.shape[2]
    experts = 2 * side * side
    lines = 2 * side
    rows = lines * lines
    anywhere = pl.BlockSpec(memory_space=pl.ANY)
    dma = pltpu.SemaphoreType.DMA
    vmem = pltpu.VMEM
    return pl.pallas_call(
        functools.partial(kernel, side, reps),
        out_shape=jax.ShapeDtypeStruct((toks, width), BF16),
        in_specs=[anywhere] * 5,
        out_specs=pl.BlockSpec(memory_space=pltpu.VMEM),
        scratch_shapes=[
            vmem((top, toks), jnp.int32),
            vmem((top, toks), F32),
            vmem((width, ff), BF16),
            vmem((ff, width), BF16),
            vmem((side, toks, width + experts), BF16),
            vmem((lines, lines, width), BF16),
            vmem((lines, lines, width), BF16),
            vmem((reps, rows // reps, ff), BF16),
            vmem((reps, rows // reps, ff), BF16),
            vmem((reps, rows // reps, ff), BF16),
            vmem((rows, width), F32),
            vmem((lines, lines, width), BF16),
            vmem((lines, lines, width), BF16),
            vmem((side, toks, width), BF16),
            vmem((side, toks, width), BF16),
            dma((5,)),
            dma((side,)), dma((side,)),
            dma((lines,)), dma((lines,)),
            dma((reps, chunks)), dma((reps, chunks)),
            dma((reps, chunks)), dma((reps, chunks)),
            dma((lines,)), dma((lines,)),
            dma((side,)), dma((side,)),
        ],
        compiler_params=pltpu.CompilerParams(
            collective_id=0, has_side_effects=True, vmem_limit_bytes=56 * 1024 * 1024),
    )(expert_ids.T, gate_weights.T, tokens, up_weight, down_weight)


def solution(mesh):
    side = round((mesh.shape["ep"] // 2) ** 0.5)
    placed = (
        P("ep", "rep"),
        P("ep", None),
        P("ep", None),
        P("ep", "rep", None),
        P("ep", None, "rep"),
    )
    return jax.shard_map(
        functools.partial(local, side, mesh.shape["rep"], 4),
        mesh=mesh, in_specs=placed, out_specs=P("ep", "rep"), check_vma=False
    )
```

```python
import functools

import jax
import jax.numpy as jnp
from jax import lax
from jax.experimental import pallas as pl
from jax.experimental.pallas import tpu as pltpu
from jax.sharding import PartitionSpec as P

MESH = pl.DeviceIdType.MESH
F32, BF16 = jnp.float32, jnp.bfloat16
PARTS = 2
CHUNKS = 1


def far_first(n):
    return [n // 2 + (-(k + 1) // 2 if k % 2 else k // 2) for k in range(n)]


def dot(a, b, ca, cb):
    return lax.dot_general(a, b, (((ca,), (cb,)), ((), ())), preferred_element_type=F32)


def iota(shape, dim):
    return lax.broadcasted_iota(jnp.int32, shape, dim)


def kernel(
    side, reps, ids_hbm, gates_hbm, tok_hbm, up_hbm, down_hbm, out_ref,
    ids_v, gates_v, up_v, down_v, told, picked, inbound, part, gathered, hid,
    sent, back, mixed, shares, weight,
    s_load, s_tok, r_tok, s_pick, r_pick, s_part, r_part, s_hid, r_hid, s_out, r_out, s_mix, r_mix,
):
    top, toks = ids_v.shape
    experts = 2 * side * side
    width = tok_hbm.shape[1]
    ffc = up_v.shape[1] // CHUNKS
    lines = 2 * side
    held = side * toks
    e = lax.axis_index("ep")
    x = lax.axis_index("rep")
    y, z, c = e // lines, (e // 2) % side, e % 2
    p, q = y * (1 - c) + z * c, z * (1 - c) + y * c
    sp = lines * (1 - c) + 2 * c
    sq = 2 * (1 - c) + lines * c
    order = far_first(side)
    half = side // 2
    place = order[half:] + order[:half]
    blocks = [(s, other) for s in order for other in range(2)]
    per_group = lines // PARTS
    lot_rows = 2 * half
    rows = per_group * lot_rows
    per = rows // reps
    streams = range(2)
    parts = [range(PARTS)[::-1], range(PARTS)]
    groups = [(h, k) for h in streams for k in parts[h]]

    def off(v, s, n):
        return lax.rem(v + s % n, n)

    barrier = pltpu.get_barrier_semaphore()

    def greet(ep, rep):
        pl.semaphore_signal(barrier, inc=1, device_id=(ep, rep), device_id_type=MESH)

    for s in order[:-1]:
        for core in range(2):
            greet(y * lines + off(z, s, side) * 2 + core, x)
            greet(off(y, s, side) * lines + z * 2 + core, x)
    greet(e + 1 - 2 * c, x)
    rep_order = far_first(reps)[:-1]
    for s in rep_order:
        greet(e, off(x, s, reps))

    loads = [
        pltpu.make_async_copy(ids_hbm, ids_v, s_load.at[0]),
        pltpu.make_async_copy(gates_hbm, gates_v, s_load.at[1]),
        pltpu.make_async_copy(tok_hbm, told.at[half - 1, :, pl.ds(0, width)], s_load.at[2]),
        pltpu.make_async_copy(up_hbm.at[0], up_v, s_load.at[3]),
        pltpu.make_async_copy(down_hbm.at[0], down_v, s_load.at[4]),
    ]
    for load in loads:
        load.start()

    loads[0].wait()
    loads[1].wait()
    ids, gates = ids_v[...], gates_v[...]
    which = iota((experts, toks), 0)
    named = jnp.zeros((experts, toks), F32)
    gate = jnp.zeros((experts, toks), F32)
    for k in range(top):
        same = which == ids[k:k + 1, :]
        named = jnp.where(same, 1.0, named)
        gate = jnp.where(same, gates[k:k + 1, :], gate)
    earlier = (iota((toks, toks), 0) < iota((toks, toks), 1)).astype(BF16)
    rank = dot(named.astype(BF16), earlier, 1, 0)
    code = jnp.where(rank > 0.5, -gate, gate).astype(BF16)
    eye = (iota((experts, experts), 0) == iota((experts, experts), 1)).astype(BF16)
    told[half - 1, :, width:] = dot(code, eye, 0, 0).astype(BF16)
    loads[2].wait()
    pl.semaphore_wait(barrier, 4 * (side - 1) + 1 + reps - 1)

    started = []

    def send(src, dst, s_sem, r_sem, ep, rep):
        copy = pltpu.make_async_remote_copy(
            src_ref=src, dst_ref=dst, send_sem=s_sem, recv_sem=r_sem, device_id=(ep, rep), device_id_type=MESH)
        copy.start()
        started.append(copy)

    def arrival(ref, sem):
        pltpu.make_async_copy(ref, ref, sem).wait()

    own = half - 1
    for i, s in enumerate(place):
        if i == own:
            continue
        send(told.at[own], told.at[i], s_tok.at[i], r_tok.at[i], off(p, s, side) * sp + q * sq + c, x)

    def expert_of(row, first):
        block = first + row // lot_rows
        k = block // 2
        s = side // 2 + jnp.where(k % 2 == 1, -((k + 1) // 2), k // 2)
        return p * sp + lax.rem(q + s, side) * sq + jnp.where(block % 2 == 1, 1 - c, c)

    held = half * toks
    row, tok = iota((rows, held), 0), iota((rows, held), 1)
    mine = (row % lot_rows) // 2 == tok // toks
    sign = jnp.where(mine, (1 - 2 * (row % 2)).astype(F32), 0.0)
    for h in streams:
        mates = slice(h * half, (h + 1) * half)
        for i in range(h * half, (h + 1) * half):
            if i != own:
                arrival(told.at[i], r_tok.at[i])
        codes = told[mates, :, width:].reshape(held, experts)
        have = told[mates, :, :width].reshape(held, width)
        for k in parts[h]:
            sel = (expert_of(iota((rows, experts), 0), k * per_group) == iota((rows, experts), 1)).astype(BF16)
            pick = jnp.where(dot(sel, codes, 1, 1) * sign > 0.0, 1.0, 0.0).astype(BF16)
            lot = dot(pick, have, 1, 0).reshape(per_group, lot_rows, width).astype(BF16)
            picked[h, k * per_group:(k + 1) * per_group] = lot
            for j in range(k * per_group, (k + 1) * per_group):
                s, other = blocks[j]
                if (s, other) == (0, 0):
                    inbound[h, j] = lot[j - k * per_group]
                    continue
                core = 1 - c if other else c
                send(picked.at[h, j], inbound.at[h, j], s_pick.at[h, j], r_pick.at[h, j],
                     p * sp + off(q, s, side) * sq + core, x)

    every = lines * lot_rows
    col, tok = iota((held, every), 1), iota((held, every), 0)
    sel = (expert_of(iota((experts, every), 1), 0) == iota((experts, every), 0)).astype(BF16)
    for h in streams:
        codes = told[h * half:(h + 1) * half, :, width:].reshape(held, experts)
        value = dot(codes, sel, 1, 0) * (1 - 2 * (col % 2)).astype(F32)
        right = (value > 0.0) & ((col % lot_rows) // 2 == tok // toks)
        weight[h] = jnp.where(right, value, 0.0).astype(BF16)

    loads[3].wait()
    for g, (h, k) in enumerate(groups):
        for j in range(k * per_group, (k + 1) * per_group):
            if blocks[j] != (0, 0):
                arrival(inbound.at[h, j], r_pick.at[h, j])
        lhs = inbound[h, k * per_group:(k + 1) * per_group].astype(F32).reshape(rows, width).astype(BF16)
        for n in range(CHUNKS):
            cols = pl.ds(n * ffc, ffc)
            part[g, :, :, cols] = dot(lhs, up_v[:, cols], 1, 0).astype(BF16).reshape(reps, per, ffc)
            for s in rep_order:
                to = off(x, s, reps)
                send(part.at[g, to, :, cols], gathered.at[g, s, :, cols], s_part.at[g, s, n], r_part.at[g, s, n], e, to)

    for g in range(len(groups)):
        for n in range(CHUNKS):
            cols = pl.ds(n * ffc, ffc)
            for s in rep_order:
                arrival(gathered.at[g, s, :, cols], r_part.at[g, s, n])
            pre = part[g, x, :, cols].astype(F32)
            for s in range(1, reps):
                pre = pre + gathered[g, s, :, cols].astype(F32)
            hid[g, x, :, cols] = (pre / (1.0 + jnp.exp(-pre))).astype(BF16)
            for s in rep_order:
                send(hid.at[g, x, :, cols], hid.at[g, x, :, cols], s_hid.at[g, s, n], r_hid.at[g, s, n],
                     e, off(x, s, reps))

    loads[4].wait()
    for g, (h, k) in enumerate(groups):
        total = None
        for n in range(CHUNKS):
            cols = pl.ds(n * ffc, ffc)
            for s in rep_order:
                arrival(hid.at[g, off(x, -s, reps), :, cols], r_hid.at[g, s, n])
            term = dot(hid[g, :, :, cols].reshape(rows, ffc), down_v[cols, :], 1, 0)
            total = term if total is None else total + term
        lot = total.reshape(per_group, lot_rows, width).astype(BF16)
        sent[h, k * per_group:(k + 1) * per_group] = lot
        for j in range(k * per_group, (k + 1) * per_group):
            s, other = blocks[j]
            if (s, other) == (0, 0):
                back[h, j] = lot[j - k * per_group]
                continue
            if other:
                ep = off(p, -s, side) * sp + q * sq + 1 - c
            else:
                ep = p * sp + off(q, -s, side) * sq + c
            send(sent.at[h, j], back.at[h, j], s_out.at[h, j], r_out.at[h, j], ep, x)

    for h in streams:
        for j in range(lines):
            if blocks[j] != (0, 0):
                arrival(back.at[h, j], r_out.at[h, j])
        lot = dot(weight[h], back[h].astype(F32).reshape(every, width).astype(BF16), 1, 0)
        mixed[h * half:(h + 1) * half] = lot.astype(BF16).reshape(half, toks, width)
        for i in range(h * half, (h + 1) * half):
            if i != own:
                send(mixed.at[i], shares.at[i], s_mix.at[i], r_mix.at[i],
                     off(p, -place[i], side) * sp + q * sq + c, x)
    total = mixed[own].astype(F32)
    for i in range(side):
        if i != own:
            arrival(shares.at[i], r_mix.at[i])
            total = total + shares[i].astype(F32)
    out_ref[...] = total.astype(BF16)

    for copy in started:
        copy.wait_send()


def local(side, reps, tokens, expert_ids, gate_weights, up_weight, down_weight):
    toks, top = expert_ids.shape
    width = tokens.shape[1]
    ff = up_weight.shape[2]
    experts = 2 * side * side
    lines = 2 * side
    half = side // 2
    groups = 2 * PARTS
    per = lines * side // groups * 2 // reps
    anywhere = pl.BlockSpec(memory_space=pl.ANY)
    dma = pltpu.SemaphoreType.DMA
    vmem = pltpu.VMEM
    return pl.pallas_call(
        functools.partial(kernel, side, reps),
        out_shape=jax.ShapeDtypeStruct((toks, width), BF16),
        in_specs=[anywhere] * 5,
        out_specs=pl.BlockSpec(memory_space=pltpu.VMEM),
        scratch_shapes=[
            vmem((top, toks), jnp.int32),
            vmem((top, toks), F32),
            vmem((width, ff), BF16),
            vmem((ff, width), BF16),
            vmem((side, toks, width + experts), BF16),
            vmem((2, lines, side, width), BF16),
            vmem((2, lines, side, width), BF16),
            vmem((groups, reps, per, ff), BF16),
            vmem((groups, reps, per, ff), BF16),
            vmem((groups, reps, per, ff), BF16),
            vmem((2, lines, side, width), BF16),
            vmem((2, lines, side, width), BF16),
            vmem((side, toks, width), BF16),
            vmem((side, toks, width), BF16),
            vmem((2, half * toks, lines * side), BF16),
            dma((5,)),
            dma((side,)), dma((side,)),
            dma((2, lines)), dma((2, lines)),
            dma((groups, reps, CHUNKS)), dma((groups, reps, CHUNKS)),
            dma((groups, reps, CHUNKS)), dma((groups, reps, CHUNKS)),
            dma((2, lines)), dma((2, lines)),
            dma((side,)), dma((side,)),
        ],
        compiler_params=pltpu.CompilerParams(
            collective_id=0, has_side_effects=True, vmem_limit_bytes=40 * 1024 * 1024),
    )(*[pltpu.with_memory_space_constraint(v, pltpu.HBM) for v in (expert_ids.T, gate_weights.T, tokens, up_weight, down_weight)])


def solution(mesh):
    side = round((mesh.shape["ep"] // 2) ** 0.5)
    placed = (
        P("ep", "rep"),
        P("ep", None),
        P("ep", None),
        P("ep", "rep", None),
        P("ep", None, "rep"),
    )
    return jax.shard_map(
        functools.partial(local, side, mesh.shape["rep"]),
        mesh=mesh, in_specs=placed, out_specs=P("ep", "rep"), check_vma=False
    )
```

```python
import functools

import jax
import jax.numpy as jnp
from jax import lax
from jax.experimental import pallas as pl
from jax.experimental.pallas import tpu as pltpu
from jax.sharding import PartitionSpec as P

MESH = pl.DeviceIdType.MESH
F32, BF16 = jnp.float32, jnp.bfloat16
PARTS = 4
CHUNKS = 1


def far_first(n):
    return [n // 2 + (-(k + 1) // 2 if k % 2 else k // 2) for k in range(n)]


def dot(a, b, ca, cb):
    return lax.dot_general(a, b, (((ca,), (cb,)), ((), ())), preferred_element_type=F32)


def iota(shape, dim):
    return lax.broadcasted_iota(jnp.int32, shape, dim)


def kernel(
    side, reps, ids_hbm, gates_hbm, tok_hbm, up_hbm, down_hbm, out_ref,
    ids_v, gates_v, up_v, down_v, told, picked, inbound, part, gathered, hid,
    sent, back, mixed, shares, weight,
    s_load, s_tok, r_tok, s_pick, r_pick, s_part, r_part, s_hid, r_hid, s_out, r_out, s_mix, r_mix,
):
    top, toks = ids_v.shape
    experts = 2 * side * side
    width = tok_hbm.shape[1]
    ffc = up_v.shape[1] // CHUNKS
    lines = 2 * side
    held = side * toks
    e = lax.axis_index("ep")
    x = lax.axis_index("rep")
    y, z, c = e // lines, (e // 2) % side, e % 2
    p, q = y * (1 - c) + z * c, z * (1 - c) + y * c
    sp = lines * (1 - c) + 2 * c
    sq = 2 * (1 - c) + lines * c
    order = far_first(side)
    half = side // 2
    place = order[half:] + order[:half]
    blocks = [(s, other) for s in order for other in range(2)]
    per_group = lines // PARTS
    lot_rows = 2 * half
    rows = per_group * lot_rows
    per = rows // reps
    streams = range(2)
    parts = [range(PARTS)[::-1], range(PARTS)]
    groups = [(h, k) for h in streams for k in parts[h]]

    def off(v, s, n):
        return lax.rem(v + s % n, n)

    barrier = pltpu.get_barrier_semaphore()

    def greet(ep, rep):
        pl.semaphore_signal(barrier, inc=1, device_id=(ep, rep), device_id_type=MESH)

    for s in order[:-1]:
        for core in range(2):
            greet(y * lines + off(z, s, side) * 2 + core, x)
            greet(off(y, s, side) * lines + z * 2 + core, x)
    greet(e + 1 - 2 * c, x)
    rep_order = far_first(reps)[:-1]
    for s in rep_order:
        greet(e, off(x, s, reps))

    loads = [
        pltpu.make_async_copy(ids_hbm, ids_v, s_load.at[0]),
        pltpu.make_async_copy(gates_hbm, gates_v, s_load.at[1]),
        pltpu.make_async_copy(tok_hbm, told.at[half - 1, :, pl.ds(0, width)], s_load.at[2]),
        pltpu.make_async_copy(up_hbm.at[0], up_v, s_load.at[3]),
        pltpu.make_async_copy(down_hbm.at[0], down_v, s_load.at[4]),
    ]
    for load in loads:
        load.start()

    loads[0].wait()
    loads[1].wait()
    ids, gates = ids_v[...], gates_v[...]
    which = iota((experts, toks), 0)
    named = jnp.zeros((experts, toks), F32)
    gate = jnp.zeros((experts, toks), F32)
    for k in range(top):
        same = which == ids[k:k + 1, :]
        named = jnp.where(same, 1.0, named)
        gate = jnp.where(same, gates[k:k + 1, :], gate)
    earlier = (iota((toks, toks), 0) < iota((toks, toks), 1)).astype(BF16)
    rank = dot(named.astype(BF16), earlier, 1, 0)
    code = jnp.where(rank > 0.5, -gate, gate).astype(BF16)
    eye = (iota((experts, experts), 0) == iota((experts, experts), 1)).astype(BF16)
    told[half - 1, :, width:] = dot(code, eye, 0, 0).astype(BF16)
    loads[2].wait()
    pl.semaphore_wait(barrier, 4 * (side - 1) + 1 + reps - 1)

    started = []

    def send(src, dst, s_sem, r_sem, ep, rep):
        copy = pltpu.make_async_remote_copy(
            src_ref=src, dst_ref=dst, send_sem=s_sem, recv_sem=r_sem, device_id=(ep, rep), device_id_type=MESH)
        copy.start()
        started.append(copy)

    def arrival(ref, sem):
        pltpu.make_async_copy(ref, ref, sem).wait()

    own = half - 1
    for i, s in enumerate(place):
        if i == own:
            continue
        send(told.at[own], told.at[i], s_tok.at[i], r_tok.at[i], off(p, s, side) * sp + q * sq + c, x)

    def expert_of(row, first):
        block = first + row // lot_rows
        k = block // 2
        s = side // 2 + jnp.where(k % 2 == 1, -((k + 1) // 2), k // 2)
        return p * sp + lax.rem(q + s, side) * sq + jnp.where(block % 2 == 1, 1 - c, c)

    held = half * toks
    row, tok = iota((rows, held), 0), iota((rows, held), 1)
    mine = (row % lot_rows) // 2 == tok // toks
    sign = jnp.where(mine, (1 - 2 * (row % 2)).astype(F32), 0.0)
    for h in streams:
        mates = slice(h * half, (h + 1) * half)
        for i in range(h * half, (h + 1) * half):
            if i != own:
                arrival(told.at[i], r_tok.at[i])
        codes = told[mates, :, width:].reshape(held, experts)
        have = told[mates, :, :width].reshape(held, width)
        for k in parts[h]:
            sel = (expert_of(iota((rows, experts), 0), k * per_group) == iota((rows, experts), 1)).astype(BF16)
            pick = jnp.where(dot(sel, codes, 1, 1) * sign > 0.0, 1.0, 0.0).astype(BF16)
            lot = dot(pick, have, 1, 0).reshape(per_group, lot_rows, width).astype(BF16)
            picked[h, k * per_group:(k + 1) * per_group] = lot
            for j in range(k * per_group, (k + 1) * per_group):
                s, other = blocks[j]
                if (s, other) == (0, 0):
                    inbound[h, j] = lot[j - k * per_group]
                    continue
                core = 1 - c if other else c
                send(picked.at[h, j], inbound.at[h, j], s_pick.at[h, j], r_pick.at[h, j],
                     p * sp + off(q, s, side) * sq + core, x)

    every = lines * lot_rows
    col, tok = iota((held, every), 1), iota((held, every), 0)
    sel = (expert_of(iota((experts, every), 1), 0) == iota((experts, every), 0)).astype(BF16)
    for h in streams:
        codes = told[h * half:(h + 1) * half, :, width:].reshape(held, experts)
        value = dot(codes, sel, 1, 0) * (1 - 2 * (col % 2)).astype(F32)
        right = (value > 0.0) & ((col % lot_rows) // 2 == tok // toks)
        weight[h] = jnp.where(right, value, 0.0).astype(BF16)

    loads[3].wait()

    def up(g):
        h, k = groups[g]
        for j in range(k * per_group, (k + 1) * per_group):
            if blocks[j] != (0, 0):
                arrival(inbound.at[h, j], r_pick.at[h, j])
        lhs = inbound[h, k * per_group:(k + 1) * per_group].astype(F32).reshape(rows, width).astype(BF16)
        for n in range(CHUNKS):
            cols = pl.ds(n * ffc, ffc)
            part[g, :, :, cols] = dot(lhs, up_v[:, cols], 1, 0).reshape(reps, per, ffc).astype(BF16)
            for s in rep_order:
                to = off(x, s, reps)
                send(part.at[g, to, :, cols], gathered.at[g, s, :, cols], s_part.at[g, s, n], r_part.at[g, s, n], e, to)

    def act(g):
        for n in range(CHUNKS):
            cols = pl.ds(n * ffc, ffc)
            for s in rep_order:
                arrival(gathered.at[g, s, :, cols], r_part.at[g, s, n])
            pre = part[g, x, :, cols].astype(F32)
            for s in range(1, reps):
                pre = pre + gathered[g, s, :, cols].astype(F32)
            hid[g, x, :, cols] = (pre / (1.0 + jnp.exp(-pre))).astype(BF16)
            for s in rep_order:
                send(hid.at[g, x, :, cols], hid.at[g, x, :, cols], s_hid.at[g, s, n], r_hid.at[g, s, n],
                     e, off(x, s, reps))

    def down(g):
        h, k = groups[g]
        total = None
        for n in range(CHUNKS):
            cols = pl.ds(n * ffc, ffc)
            for s in rep_order:
                arrival(hid.at[g, off(x, -s, reps), :, cols], r_hid.at[g, s, n])
            term = dot(hid[g, :, :, cols].astype(F32).reshape(rows, ffc).astype(BF16), down_v[cols, :], 1, 0)
            total = term if total is None else total + term
        lot = total.reshape(per_group, lot_rows, width).astype(BF16)
        sent[h, k * per_group:(k + 1) * per_group] = lot
        for j in range(k * per_group, (k + 1) * per_group):
            s, other = blocks[j]
            if (s, other) == (0, 0):
                back[h, j] = lot[j - k * per_group]
                continue
            if other:
                ep = off(p, -s, side) * sp + q * sq + 1 - c
            else:
                ep = p * sp + off(q, -s, side) * sq + c
            send(sent.at[h, j], back.at[h, j], s_out.at[h, j], r_out.at[h, j], ep, x)

    loads[4].wait()
    for step in (up, act, down):
        for g in range(len(groups)):
            step(g)

    for h in streams:
        for j in range(lines):
            if blocks[j] != (0, 0):
                arrival(back.at[h, j], r_out.at[h, j])
        lot = dot(weight[h], back[h].astype(F32).reshape(every, width).astype(BF16), 1, 0)
        mixed[h * half:(h + 1) * half] = lot.astype(BF16).reshape(half, toks, width)
        for i in range(h * half, (h + 1) * half):
            if i != own:
                send(mixed.at[i], shares.at[i], s_mix.at[i], r_mix.at[i],
                     off(p, -place[i], side) * sp + q * sq + c, x)
    for copy in started[:-(side - 1)]:
        copy.wait_send()
    total = mixed[own].astype(F32)
    for i in range(side):
        if i != own:
            arrival(shares.at[i], r_mix.at[i])
            total = total + shares[i].astype(F32)
    out_ref[...] = total.astype(BF16)

    for copy in started[-(side - 1):]:
        copy.wait_send()


def local(side, reps, tokens, expert_ids, gate_weights, up_weight, down_weight):
    toks, top = expert_ids.shape
    width = tokens.shape[1]
    ff = up_weight.shape[2]
    experts = 2 * side * side
    lines = 2 * side
    half = side // 2
    groups = 2 * PARTS
    per = lines * side // groups * 2 // reps
    anywhere = pl.BlockSpec(memory_space=pl.ANY)
    dma = pltpu.SemaphoreType.DMA
    vmem = pltpu.VMEM
    return pl.pallas_call(
        functools.partial(kernel, side, reps),
        out_shape=jax.ShapeDtypeStruct((toks, width), BF16),
        in_specs=[anywhere] * 5,
        out_specs=pl.BlockSpec(memory_space=pltpu.VMEM),
        scratch_shapes=[
            vmem((top, toks), jnp.int32),
            vmem((top, toks), F32),
            vmem((width, ff), BF16),
            vmem((ff, width), BF16),
            vmem((side, toks, width + experts), BF16),
            vmem((2, lines, side, width), BF16),
            vmem((2, lines, side, width), BF16),
            vmem((groups, reps, per, ff), BF16),
            vmem((groups, reps, per, ff), BF16),
            vmem((groups, reps, per, ff), BF16),
            vmem((2, lines, side, width), BF16),
            vmem((2, lines, side, width), BF16),
            vmem((side, toks, width), BF16),
            vmem((side, toks, width), BF16),
            vmem((2, half * toks, lines * side), BF16),
            dma((5,)),
            dma((side,)), dma((side,)),
            dma((2, lines)), dma((2, lines)),
            dma((groups, reps, CHUNKS)), dma((groups, reps, CHUNKS)),
            dma((groups, reps, CHUNKS)), dma((groups, reps, CHUNKS)),
            dma((2, lines)), dma((2, lines)),
            dma((side,)), dma((side,)),
        ],
        compiler_params=pltpu.CompilerParams(
            collective_id=0, has_side_effects=True, vmem_limit_bytes=40 * 1024 * 1024),
    )(*[pltpu.with_memory_space_constraint(v, pltpu.HBM) for v in (expert_ids.T, gate_weights.T, tokens, up_weight, down_weight)])


def solution(mesh):
    side = round((mesh.shape["ep"] // 2) ** 0.5)
    placed = (
        P("ep", "rep"),
        P("ep", None),
        P("ep", None),
        P("ep", "rep", None),
        P("ep", None, "rep"),
    )
    return jax.shard_map(
        functools.partial(local, side, mesh.shape["rep"]),
        mesh=mesh, in_specs=placed, out_specs=P("ep", "rep"), check_vma=False
    )
```

```python
import functools

import jax
import jax.numpy as jnp
from jax import lax
from jax.experimental import pallas as pl
from jax.experimental.pallas import tpu as pltpu
from jax.sharding import PartitionSpec as P

MESH = pl.DeviceIdType.MESH
F32, BF16 = jnp.float32, jnp.bfloat16
PARTS = 4
CHUNKS = 1


def far_first(n):
    return [n // 2 + (-(k + 1) // 2 if k % 2 else k // 2) for k in range(n)]


def dot(a, b, ca, cb):
    return lax.dot_general(a, b, (((ca,), (cb,)), ((), ())), preferred_element_type=F32)


def iota(shape, dim):
    return lax.broadcasted_iota(jnp.int32, shape, dim)


def kernel(
    side, reps, ids_hbm, gates_hbm, tok_hbm, up_hbm, down_hbm, out_ref,
    ids_v, gates_v, up_v, down_v, told, picked, inbound, part, gathered, hid,
    sent, back, mixed, shares, weight,
    s_load, s_tok, r_tok, s_pick, r_pick, s_part, r_part, s_hid, r_hid, s_out, r_out, s_mix, r_mix,
):
    top, toks = ids_v.shape
    experts = 2 * side * side
    width = tok_hbm.shape[1]
    ffc = up_v.shape[1] // CHUNKS
    lines = 2 * side
    held = side * toks
    e = lax.axis_index("ep")
    x = lax.axis_index("rep")
    y, z, c = e // lines, (e // 2) % side, e % 2
    p, q = y * (1 - c) + z * c, z * (1 - c) + y * c
    sp = lines * (1 - c) + 2 * c
    sq = 2 * (1 - c) + lines * c
    order = far_first(side)
    half = side // 2
    place = order[half:] + order[:half]
    blocks = [(s, other) for s in order for other in range(2)]
    per_group = lines // PARTS
    lot_rows = 2 * half
    rows = per_group * lot_rows
    per = rows // reps
    streams = range(2)
    parts = [range(PARTS)[::-1], range(PARTS)]
    groups = [(h, k) for h in streams for k in parts[h]]

    def off(v, s, n):
        return lax.rem(v + s % n, n)

    loads = [
        pltpu.make_async_copy(ids_hbm, ids_v, s_load.at[0]),
        pltpu.make_async_copy(gates_hbm, gates_v, s_load.at[1]),
        pltpu.make_async_copy(tok_hbm, told.at[half - 1, :, pl.ds(0, width)], s_load.at[2]),
        pltpu.make_async_copy(up_hbm.at[0], up_v, s_load.at[3]),
        pltpu.make_async_copy(down_hbm.at[0], down_v, s_load.at[4]),
    ]
    for load in loads[:3]:
        load.start()

    barrier = pltpu.get_barrier_semaphore()

    def greet(ep, rep):
        pl.semaphore_signal(barrier, inc=1, device_id=(ep, rep), device_id_type=MESH)

    for s in order[:-1]:
        for core in range(2):
            greet(y * lines + off(z, s, side) * 2 + core, x)
            greet(off(y, s, side) * lines + z * 2 + core, x)
    greet(e + 1 - 2 * c, x)
    rep_order = far_first(reps)[:-1]
    for s in rep_order:
        greet(e, off(x, s, reps))

    for load in loads[3:]:
        load.start()

    loads[0].wait()
    loads[1].wait()
    ids, gates = ids_v[...], gates_v[...]
    which = iota((experts, toks), 0)
    named = jnp.zeros((experts, toks), F32)
    gate = jnp.zeros((experts, toks), F32)
    for k in range(top):
        same = which == ids[k:k + 1, :]
        named = jnp.where(same, 1.0, named)
        gate = jnp.where(same, gates[k:k + 1, :], gate)
    earlier = (iota((toks, toks), 0) < iota((toks, toks), 1)).astype(BF16)
    rank = dot(named.astype(BF16), earlier, 1, 0)
    code = jnp.where(rank > 0.5, -gate, gate).astype(BF16)
    eye = (iota((experts, experts), 0) == iota((experts, experts), 1)).astype(BF16)
    told[half - 1, :, width:] = dot(code, eye, 0, 0).astype(BF16)
    loads[2].wait()
    pl.semaphore_wait(barrier, 4 * (side - 1) + 1 + reps - 1)

    started = []

    def send(src, dst, s_sem, r_sem, ep, rep):
        copy = pltpu.make_async_remote_copy(
            src_ref=src, dst_ref=dst, send_sem=s_sem, recv_sem=r_sem, device_id=(ep, rep), device_id_type=MESH)
        copy.start()
        started.append(copy)

    def arrival(ref, sem):
        pltpu.make_async_copy(ref, ref, sem).wait()

    own = half - 1
    for i, s in enumerate(place):
        if i == own:
            continue
        send(told.at[own], told.at[i], s_tok.at[i], r_tok.at[i], off(p, s, side) * sp + q * sq + c, x)

    def expert_of(row, first):
        block = first + row // lot_rows
        k = block // 2
        s = side // 2 + jnp.where(k % 2 == 1, -((k + 1) // 2), k // 2)
        return p * sp + lax.rem(q + s, side) * sq + jnp.where(block % 2 == 1, 1 - c, c)

    held = half * toks
    row, tok = iota((rows, held), 0), iota((rows, held), 1)
    mine = (row % lot_rows) // 2 == tok // toks
    sign = jnp.where(mine, (1 - 2 * (row % 2)).astype(F32), 0.0)
    for h in streams:
        mates = slice(h * half, (h + 1) * half)
        for i in range(h * half, (h + 1) * half):
            if i != own:
                arrival(told.at[i], r_tok.at[i])
        codes = told[mates, :, width:].reshape(held, experts)
        have = told[mates, :, :width].reshape(held, width)
        for k in parts[h]:
            sel = (expert_of(iota((rows, experts), 0), k * per_group) == iota((rows, experts), 1)).astype(BF16)
            pick = jnp.where(dot(sel, codes, 1, 1) * sign > 0.0, 1.0, 0.0).astype(BF16)
            lot = dot(pick, have, 1, 0).reshape(per_group, lot_rows, width).astype(BF16)
            picked[h, k * per_group:(k + 1) * per_group] = lot
            for j in range(k * per_group, (k + 1) * per_group):
                s, other = blocks[j]
                if (s, other) == (0, 0):
                    inbound[h, j] = lot[j - k * per_group]
                    continue
                core = 1 - c if other else c
                send(picked.at[h, j], inbound.at[h, j], s_pick.at[h, j], r_pick.at[h, j],
                     p * sp + off(q, s, side) * sq + core, x)

    every = lines * lot_rows
    col, tok = iota((held, every), 1), iota((held, every), 0)
    sel = (expert_of(iota((experts, every), 1), 0) == iota((experts, every), 0)).astype(BF16)
    for h in streams:
        codes = told[h * half:(h + 1) * half, :, width:].reshape(held, experts)
        value = dot(codes, sel, 1, 0) * (1 - 2 * (col % 2)).astype(F32)
        right = (value > 0.0) & ((col % lot_rows) // 2 == tok // toks)
        weight[h] = jnp.where(right, value, 0.0).astype(BF16)

    loads[3].wait()

    def up(g):
        h, k = groups[g]
        for j in range(k * per_group, (k + 1) * per_group):
            if blocks[j] != (0, 0):
                arrival(inbound.at[h, j], r_pick.at[h, j])
        lhs = inbound[h, k * per_group:(k + 1) * per_group].astype(F32).reshape(rows, width).astype(BF16)
        for n in range(CHUNKS):
            cols = pl.ds(n * ffc, ffc)
            part[g, :, :, cols] = dot(lhs, up_v[:, cols], 1, 0).reshape(reps, per, ffc).astype(BF16)
            for s in rep_order:
                to = off(x, s, reps)
                send(part.at[g, to, :, cols], gathered.at[g, s, :, cols], s_part.at[g, s, n], r_part.at[g, s, n], e, to)

    def act(g):
        for n in range(CHUNKS):
            cols = pl.ds(n * ffc, ffc)
            for s in rep_order:
                arrival(gathered.at[g, s, :, cols], r_part.at[g, s, n])
            pre = part[g, x, :, cols].astype(F32)
            for s in range(1, reps):
                pre = pre + gathered[g, s, :, cols].astype(F32)
            hid[g, x, :, cols] = (pre / (1.0 + jnp.exp(-pre))).astype(BF16)
            for s in rep_order:
                send(hid.at[g, x, :, cols], hid.at[g, x, :, cols], s_hid.at[g, s, n], r_hid.at[g, s, n],
                     e, off(x, s, reps))

    def down(g):
        h, k = groups[g]
        total = None
        for n in range(CHUNKS):
            cols = pl.ds(n * ffc, ffc)
            for s in rep_order:
                arrival(hid.at[g, off(x, -s, reps), :, cols], r_hid.at[g, s, n])
            term = dot(hid[g, :, :, cols].astype(F32).reshape(rows, ffc).astype(BF16), down_v[cols, :], 1, 0)
            total = term if total is None else total + term
        lot = total.reshape(per_group, lot_rows, width).astype(BF16)
        sent[h, k * per_group:(k + 1) * per_group] = lot
        for j in range(k * per_group, (k + 1) * per_group):
            s, other = blocks[j]
            if (s, other) == (0, 0):
                back[h, j] = lot[j - k * per_group]
                continue
            if other:
                ep = off(p, -s, side) * sp + q * sq + 1 - c
            else:
                ep = p * sp + off(q, -s, side) * sq + c
            send(sent.at[h, j], back.at[h, j], s_out.at[h, j], r_out.at[h, j], ep, x)

    loads[4].wait()
    for step in (up, act, down):
        for g in range(len(groups)):
            step(g)

    for h in streams:
        for j in range(lines):
            if blocks[j] != (0, 0):
                arrival(back.at[h, j], r_out.at[h, j])
        lot = dot(weight[h], back[h].astype(F32).reshape(every, width).astype(BF16), 1, 0)
        mixed[h * half:(h + 1) * half] = lot.astype(BF16).reshape(half, toks, width)
        for i in range(h * half, (h + 1) * half):
            if i != own:
                send(mixed.at[i], shares.at[i], s_mix.at[i], r_mix.at[i],
                     off(p, -place[i], side) * sp + q * sq + c, x)
    for copy in started[:-(side - 1)]:
        copy.wait_send()
    total = mixed[own].astype(F32)
    for i in range(side):
        if i != own:
            arrival(shares.at[i], r_mix.at[i])
            total = total + shares[i].astype(F32)
    out_ref[...] = total.astype(BF16)

    for copy in started[-(side - 1):]:
        copy.wait_send()


def local(side, reps, tokens, expert_ids, gate_weights, up_weight, down_weight):
    toks, top = expert_ids.shape
    width = tokens.shape[1]
    ff = up_weight.shape[2]
    experts = 2 * side * side
    lines = 2 * side
    half = side // 2
    groups = 2 * PARTS
    per = lines * side // groups * 2 // reps
    anywhere = pl.BlockSpec(memory_space=pl.ANY)
    dma = pltpu.SemaphoreType.DMA
    vmem = pltpu.VMEM
    return pl.pallas_call(
        functools.partial(kernel, side, reps),
        out_shape=jax.ShapeDtypeStruct((toks, width), BF16),
        in_specs=[anywhere] * 5,
        out_specs=pl.BlockSpec(memory_space=pltpu.VMEM),
        scratch_shapes=[
            vmem((top, toks), jnp.int32),
            vmem((top, toks), F32),
            vmem((width, ff), BF16),
            vmem((ff, width), BF16),
            vmem((side, toks, width + experts), BF16),
            vmem((2, lines, side, width), BF16),
            vmem((2, lines, side, width), BF16),
            vmem((groups, reps, per, ff), BF16),
            vmem((groups, reps, per, ff), BF16),
            vmem((groups, reps, per, ff), BF16),
            vmem((2, lines, side, width), BF16),
            vmem((2, lines, side, width), BF16),
            vmem((side, toks, width), BF16),
            vmem((side, toks, width), BF16),
            vmem((2, half * toks, lines * side), BF16),
            dma((5,)),
            dma((side,)), dma((side,)),
            dma((2, lines)), dma((2, lines)),
            dma((groups, reps, CHUNKS)), dma((groups, reps, CHUNKS)),
            dma((groups, reps, CHUNKS)), dma((groups, reps, CHUNKS)),
            dma((2, lines)), dma((2, lines)),
            dma((side,)), dma((side,)),
        ],
        compiler_params=pltpu.CompilerParams(
            collective_id=0, has_side_effects=True, vmem_limit_bytes=40 * 1024 * 1024),
    )(*[pltpu.with_memory_space_constraint(v, pltpu.HBM) for v in (expert_ids.T, gate_weights.T, tokens, up_weight, down_weight)])


def solution(mesh):
    side = round((mesh.shape["ep"] // 2) ** 0.5)
    placed = (
        P("ep", "rep"),
        P("ep", None),
        P("ep", None),
        P("ep", "rep", None),
        P("ep", None, "rep"),
    )
    return jax.shard_map(
        functools.partial(local, side, mesh.shape["rep"]),
        mesh=mesh, in_specs=placed, out_specs=P("ep", "rep"), check_vma=False
    )
```
